256 devices in a mesh: pp: 8 (over y, core), ep: 32 (over x, z).
Axes of the slice: x: 4, y: 4, z: 8, core: 2. Of those that a mesh axis runs over, the one named last changes fastest.
Arguments:
- fwd_in: bfloat16 [8, 4096, 3584], P('pp', 'ep'), may hold values from -6 to 6
- fwd_ids: int32 [8, 4096, 1], P('pp', 'ep'), may hold values from 0 to 7; in each aligned block of 128 rows (0 to 127, 128 to 255, ..., all dimensions but the last counted through in order) at most 20 rows name the same one
- saved_in: bfloat16 [8, 4096, 3584], P('pp', 'ep'), may hold values from -6 to 6
- bwd_ids: int32 [8, 4096, 1], P('pp', 'ep'), may hold values from 0 to 7; in each aligned block of 128 rows (0 to 127, 128 to 255, ..., all dimensions but the last counted through in order) at most 20 rows name the same one
- grad_in: bfloat16 [8, 4096, 3584], P('pp', 'ep'), may hold values from -6 to 6
- router: float32 [8, 3584, 8], P('pp'), may hold values from -0.09375 to 0.09375
- w_gate: bfloat16 [8, 3584, 8192], P('pp', None, 'ep'), may hold values from -0.09375 to 0.09375
- w_up: bfloat16 [8, 3584, 8192], P('pp', None, 'ep'), may hold values from -0.09375 to 0.09375
- w_down: bfloat16 [8, 8192, 3584], P('pp', 'ep'), may hold values from -0.1875 to 0.1875
Outputs:
- fwd_next: bfloat16 [8, 4096, 3584], P('pp', 'ep')
- grad_next: bfloat16 [8, 4096, 3584], P('pp', 'ep')
The draws below stay inside these ranges and needn't reach their ends.
Inputs may be any that keep to these rules, and one draw needn't show every extreme that they name: `fwd_ids`: within the 128 tokens of one device's aligned block, no expert is chosen more than 20 times; some block chooses some expert exactly 20 times. `bwd_ids`: as for fwd_ids.
All inputs are finite; a program needn't handle non-finite values.
Results may differ from the reference program's by a relative error of at most 0.011.
Values may be sent and summed in bfloat16 or wider, within the bound.
A program may use at most 128 MiB of HBM per device.

```python
import math
import jax
import jax.numpy as jnp
import numpy as np
from jax import lax

D = 3584
FF = 1024
EXPERTS = 8
TOPK = 1
TOK_DEV = 128
SPAN = 4
FF_DEV = 256
CAP = 20
TOKENS = 4096
N_PP = 8
N_EP = 32


def block_scale(stream_key, dims, shards, least, largest):
    def one(axis_at, blocks):
        steps = jax.random.uniform(jax.random.fold_in(jax.random.fold_in(stream_key, 6), axis_at), (blocks,), jnp.float32, least / len(shards), largest / len(shards))
        return jnp.repeat(jnp.exp(steps), dims[axis_at] // blocks).reshape((-1,) + (1,) * (len(dims) - axis_at - 1))

    loudness = one(*shards[0])
    for cut in shards[1:]:
        loudness = loudness * one(*cut)
    return loudness


def routed_block(own_key, own, number, rows, count, top, bound, lean):
    order = jax.random.permutation(own_key, count)
    crowded, ordinary = shares(count, rows * top, bound, lean, True), shares(count, rows * top, bound, lean, False)
    places = jnp.arange(count)

    def named(lengths, offset_by):
        used = int((lengths > 0).sum())
        fixed = max(1, used // 4)
        passed = fixed + (places - fixed + offset_by * (used - fixed)) % max(1, count - fixed)
        return jnp.zeros((count,), jnp.int32).at[order[jnp.where(places < fixed, places, passed)]].set(jnp.asarray(lengths, jnp.int32))

    lengths = jnp.where(number % 4 == 0, named(crowded, number // 4), named(ordinary, number - number // 4 - 1))
    mixed = jax.random.permutation(jax.random.fold_in(own, 3), count)
    giver, receiver = mixed[0:count // 2 * 2:2], mixed[1:count // 2 * 2:2]
    slack = jnp.minimum(lengths[giver] - 1, bound - lengths[receiver]) // 2
    slack = jnp.where((giver == order[0]) | (receiver == order[0]) | (lengths[receiver] == 0), 0, jnp.maximum(slack, 0))
    passed = jax.random.randint(jax.random.fold_in(own, 4), (count // 2,), 0, 1 << 20) % (slack + 1)
    lengths = lengths.at[giver].add(-passed).at[receiver].add(passed)
    labels = jnp.searchsorted(jnp.cumsum(lengths), jnp.arange(rows * top), side="right").astype(jnp.int32)
    listing = labels.reshape(top, rows).T
    listing = listing[jax.random.permutation(jax.random.fold_in(own, 1), rows)]
    offset_by = jax.random.randint(jax.random.fold_in(own, 2), (rows, 1), 0, top)
    return jnp.take_along_axis(listing, (jnp.arange(top)[None, :] + offset_by) % top, axis=1)


def shares(number_of, total, reach, lean, full):
    portions = [(1 << 20) // math.isqrt(standing ** lean) + 1 for standing in range(1, number_of + 1)]
    largest = reach if full else min(reach, max(-(-total // number_of), total * portions[0] // sum(portions)))
    least = 1 if total - largest >= number_of - 1 else 0
    counts, surplus = [largest] + [least] * (number_of - 1), total - largest - least * (number_of - 1)
    while surplus > 0:
        free = [i for i in range(1, number_of) if counts[i] < largest] or [i for i in range(1, number_of) if counts[i] < reach]
        pool, left = sum([portions[i] for i in free]), surplus
        for i in free:
            more = min(reach - counts[i], max(1, left * portions[i] // pool), surplus)
            counts[i] = counts[i] + more
            surplus = surplus - more
    return np.array(counts)


def scatter_about(stream_key, extent, scale, bound, split=(), kind=jnp.bfloat16):
    loudness = block_scale(stream_key, extent, split, -0.22, 0.18) if split else 1.0
    values = jax.random.normal(stream_key, extent, jnp.float32) * scale * loudness
    return jnp.minimum(jnp.maximum(values, -bound), bound).astype(kind)


def setup_inputs(seed: int = 0) -> dict:
    seeds = jax.random.split(jax.random.key(seed), 10)
    fwd_in = scatter_about(seeds[0], (N_PP, TOKENS, D), 1.0, 6.0, ((0, 8), (1, 32)))
    fwd_ids_keys = jax.random.split(jax.random.fold_in(seeds[1], 1), N_PP * TOKENS // TOK_DEV)
    fwd_ids_turns = jax.random.permutation(jax.random.fold_in(seeds[1], 3), N_PP * TOKENS // TOK_DEV)
    fwd_ids = jax.vmap(lambda own, number: routed_block(jax.random.fold_in(seeds[1], 2), own, number, TOK_DEV, EXPERTS, TOPK, CAP, 2))(fwd_ids_keys, fwd_ids_turns).reshape((N_PP, TOKENS, TOPK))
    saved_in = scatter_about(seeds[2], (N_PP, TOKENS, D), 1.0, 6.0, ((0, 8), (1, 32)))
    bwd_ids_keys = jax.random.split(jax.random.fold_in(seeds[3], 1), N_PP * TOKENS // TOK_DEV)
    bwd_ids_turns = jax.random.permutation(jax.random.fold_in(seeds[3], 3), N_PP * TOKENS // TOK_DEV)
    bwd_ids = jax.vmap(lambda own, number: routed_block(jax.random.fold_in(seeds[3], 2), own, number, TOK_DEV, EXPERTS, TOPK, CAP, 2))(bwd_ids_keys, bwd_ids_turns).reshape((N_PP, TOKENS, TOPK))
    grad_in = scatter_about(seeds[4], (N_PP, TOKENS, D), 1.0, 6.0, ((0, 8), (1, 32)))
    router = scatter_about(seeds[5], (N_PP, D, EXPERTS), D ** -0.5, 0.09375, ((0, 8),), jnp.float32)
    w_gate = scatter_about(seeds[6], (N_PP, D, EXPERTS * FF), D ** -0.5, 0.09375, ((0, 8), (2, 32)))
    w_up = scatter_about(seeds[7], (N_PP, D, EXPERTS * FF), D ** -0.5, 0.09375, ((0, 8), (2, 32)))
    w_down = scatter_about(seeds[8], (N_PP, EXPERTS * FF, D), FF ** -0.5, 0.1875, ((0, 8), (1, 32)))
    return {"fwd_in": fwd_in, "fwd_ids": fwd_ids, "saved_in": saved_in, "bwd_ids": bwd_ids, "grad_in": grad_in, "router": router, "w_gate": w_gate, "w_up": w_up, "w_down": w_down}


route_scale = 2.5
contract = (((1,), (1,)), ((), ()))


def slots_of(chosen):
    blocks = chosen.reshape(N_EP, TOK_DEV)
    onehot = (blocks[:, :, None] == jnp.arange(EXPERTS, dtype=jnp.int32)[None, None, :]).astype(jnp.int32)
    before = jnp.cumsum(onehot, axis=1) - onehot
    ranking = jnp.sum(before * onehot, axis=2)
    slot_index = (jnp.arange(N_EP, dtype=jnp.int32)[:, None] * CAP + ranking).reshape(-1).astype(jnp.int32)
    slot_table = jnp.full((EXPERTS, N_EP * CAP), TOKENS, jnp.int32)
    slot_table = slot_table.at[chosen, slot_index].set(jnp.arange(TOKENS, dtype=jnp.int32))
    return slot_index, slot_table


def routing_weight(tokens, router, chosen):
    logits = jnp.dot(tokens.astype(jnp.float32), router, precision=lax.Precision.HIGHEST)
    picked = jnp.take_along_axis(logits, chosen[:, None], axis=1)[:, 0]
    return route_scale * jax.nn.sigmoid(picked)


def expert_forward(row_block, gate_cols, up_cols, down_rows):
    gate_proj = jnp.dot(row_block, gate_cols, preferred_element_type=jnp.float32)
    up_proj = jnp.dot(row_block, up_cols, preferred_element_type=jnp.float32)
    hidden = (gate_proj * jax.nn.sigmoid(gate_proj) * up_proj).astype(jnp.bfloat16)
    running = jnp.zeros((row_block.shape[0], D), jnp.float32)
    for unit_block in range(SPAN):
        first_unit = unit_block * FF_DEV
        partial_sum = jnp.dot(hidden[:, first_unit:first_unit + FF_DEV], down_rows[first_unit:first_unit + FF_DEV], preferred_element_type=jnp.float32).astype(jnp.bfloat16)
        running = running + partial_sum.astype(jnp.float32)
    return running.astype(jnp.bfloat16)


def expert_backward(row_block, row_grads, gate_cols, up_cols, down_rows):
    gate_proj = jnp.dot(row_block, gate_cols, preferred_element_type=jnp.float32)
    up_proj = jnp.dot(row_block, up_cols, preferred_element_type=jnp.float32)
    d_hidden = lax.dot_general(row_grads, down_rows, contract, preferred_element_type=jnp.float32)
    sigmoid_gate = jax.nn.sigmoid(gate_proj)
    d_gate = (d_hidden * up_proj * sigmoid_gate * (1.0 + gate_proj * (1.0 - sigmoid_gate))).astype(jnp.bfloat16)
    d_up = (d_hidden * gate_proj * sigmoid_gate).astype(jnp.bfloat16)
    running = jnp.zeros((row_block.shape[0], D), jnp.float32)
    for unit_block in range(SPAN):
        first_unit = unit_block * FF_DEV
        last_unit = first_unit + FF_DEV
        partial_sum = lax.dot_general(d_gate[:, first_unit:last_unit], gate_cols[:, first_unit:last_unit], contract, preferred_element_type=jnp.float32)
        partial_sum = partial_sum + lax.dot_general(d_up[:, first_unit:last_unit], up_cols[:, first_unit:last_unit], contract, preferred_element_type=jnp.float32)
        running = running + partial_sum.astype(jnp.bfloat16).astype(jnp.float32)
    return running.astype(jnp.bfloat16)


def split_experts(w_gate, w_up, w_down):
    gate_each = w_gate.reshape(D, EXPERTS, FF).transpose(1, 0, 2)
    up_each = w_up.reshape(D, EXPERTS, FF).transpose(1, 0, 2)
    down_each = w_down.reshape(EXPERTS, FF, D)
    return gate_each, up_each, down_each


def with_zero_row(tokens):
    return jnp.concatenate([tokens, jnp.zeros((1, D), tokens.dtype)], axis=0)


def section_forward(tokens, chosen, router, w_gate, w_up, w_down):
    slot_index, slot_table = slots_of(chosen)
    weight = routing_weight(tokens, router, chosen)
    padded = with_zero_row(tokens)
    gate_each, up_each, down_each = split_experts(w_gate, w_up, w_down)

    def per_expert(inputs):
        slot_row, gate_cols, up_cols, down_rows = inputs
        return expert_forward(padded[slot_row], gate_cols, up_cols, down_rows)

    outputs = lax.map(per_expert, (slot_table, gate_each, up_each, down_each))
    expert_out = lax.optimization_barrier(outputs[chosen, slot_index]).astype(jnp.float32)
    return (tokens.astype(jnp.float32) + weight[:, None] * expert_out).astype(jnp.bfloat16)


def section_backward(saved, chosen, grads, router, w_gate, w_up, w_down):
    slot_index, slot_table = slots_of(chosen)
    weight = routing_weight(saved, router, chosen)
    weighted = (weight[:, None] * grads.astype(jnp.float32)).astype(jnp.bfloat16)
    padded = with_zero_row(saved)
    padded_grads = with_zero_row(weighted)
    gate_each, up_each, down_each = split_experts(w_gate, w_up, w_down)

    def per_expert(inputs):
        slot_row, gate_cols, up_cols, down_rows = inputs
        return expert_backward(padded[slot_row], padded_grads[slot_row], gate_cols, up_cols, down_rows)

    outputs = lax.map(per_expert, (slot_table, gate_each, up_each, down_each))
    expert_out = lax.optimization_barrier(outputs[chosen, slot_index]).astype(jnp.float32)
    return (grads.astype(jnp.float32) + expert_out).astype(jnp.bfloat16)


def reference(fwd_in, fwd_ids, saved_in, bwd_ids, grad_in, router, w_gate, w_up, w_down):
    forward_list = []
    backward_list = []
    for section_index in range(N_PP):
        forward_list.append(section_forward(fwd_in[section_index], fwd_ids[section_index, :, 0], router[section_index], w_gate[section_index], w_up[section_index], w_down[section_index]))
        backward_list.append(section_backward(saved_in[section_index], bwd_ids[section_index, :, 0], grad_in[section_index], router[section_index], w_gate[section_index], w_up[section_index], w_down[section_index]))
    fwd_next = jnp.roll(jnp.stack(forward_list), 1, axis=0)
    grad_next = jnp.roll(jnp.stack(backward_list), -1, axis=0)
    return fwd_next, grad_next
```

```python
import functools

import jax
import jax.numpy as jnp
from jax import lax
from jax.experimental import pallas as pl
from jax.experimental.pallas import tpu as pltpu
from jax.sharding import PartitionSpec as P

route_scale = 2.5
MESH = pl.DeviceIdType.MESH
f32 = jnp.float32
bf16 = jnp.bfloat16

NX = 4
NZ = 8
SPAN = 4
CAP = 20
MSG = 48
BLK = NX * CAP
OWN = 7
FROM_LEFT, FROM_RIGHT, AWAY = 7, 8, 9
B_AT = 6
B_PREP = 3
LAG = 2
F_DONE = 12
COLS = 512


def nt(a, b):
    return lax.dot_general(a, b, (((1,), (1,)), ((), ())), preferred_element_type=f32)


def nn(a, b):
    return jnp.dot(a, b, preferred_element_type=f32)


def kernel(
    pf, pb, pft, pbt, q, qt, fw, fwd, sav, wgt, grd, wg_h, wu_h, wd_h,
    out_f, out_b,
    tok, wg, wu, wd, xs, xr, inb, away, part, back, ys, yr, sec,
    ld_sem, x_ss, x_rs, in_ss, in_rs, f_ss, o_ss, o_rs, y_ss, y_rs, pp_ss, pp_rs,
):
    width = tok.shape[2]
    chunks = width // COLS
    pp = lax.axis_index("pp")
    ep = lax.axis_index("ep")
    n_pp = lax.axis_size("pp")
    x = ep // NZ
    z = ep % NZ
    h = z // SPAN
    i = z % SPAN

    def at(xx, zz):
        return {"ep": (xx % NX) * NZ + (zz + NZ) % NZ}

    right = at(x, z + 1)
    left = at(x, z - 1)
    pp_up = {"pp": (pp + 1) % n_pp}
    pp_down = {"pp": (pp + n_pp - 1) % n_pp}

    loads = [
        pltpu.make_async_copy(src, dst, ld_sem.at[j])
        for j, (src, dst) in enumerate([
            (fwd, tok.at[0]), (sav, tok.at[1]), (wgt, tok.at[2]), (grd, tok.at[3]),
            (wg_h, wg), (wu_h, wu), (wd_h, wd),
        ])
    ]
    for load in loads:
        load.start()

    barrier = pltpu.get_barrier_semaphore()
    friends = [at(x + 1, z), at(x + 2, z), at(x + 3, z), right, left, at(x, z + 2), at(x, z - 2), pp_up, pp_down]
    for friend in friends:
        pl.semaphore_signal(barrier, inc=1, device_id=friend, device_id_type=MESH)
    pl.semaphore_wait(barrier, len(friends))

    def remote(src, dst, ss, rs, dev):
        return pltpu.make_async_remote_copy(
            src_ref=src, dst_ref=dst, send_sem=ss, recv_sem=rs, device_id=dev, device_id_type=MESH
        )

    def cols(c):
        return pl.ds(pl.multiple_of(c * COLS, COLS), COLS)

    def rows48(k):
        return pl.ds(pl.multiple_of(k * MSG, 16), MSG)

    def x_copy(t, d):
        return remote(xs.at[t, d - 1], xr.at[t, rows48(x), :], x_ss.at[t, d - 1], x_rs.at[t, d - 1], at(x + d, z))

    def x_arrival(t, d):
        return remote(
            xs.at[t, d - 1], xr.at[t, rows48((x + NX - d) % NX), :], x_ss.at[t, d - 1], x_rs.at[t, d - 1], at(x + d, z)
        )

    def x_send(t, p_ref):
        for d in (2, 1, 3, 0):
            xd = (x + d) % NX

            @pl.loop(0, chunks)
            def _(c, d=d, xd=xd):
                picked = nn(p_ref[rows48(xd), :], tok[t, :, cols(c)]).astype(bf16)
                if d == 0:
                    xr[t, rows48(x), cols(c)] = picked
                else:
                    xs[t, d - 1, :, cols(c)] = picked

            if d:
                x_copy(t, d).start()

    def own_right(t):
        return remote(inb.at[t, OWN], inb.at[t, 0], in_ss.at[t, OWN, 0], in_rs.at[t, 0], right)

    def own_left(t):
        return remote(inb.at[t, OWN], inb.at[t, 6], in_ss.at[t, OWN, 1], in_rs.at[t, 6], left)

    def own_away(t):
        slot = jnp.where(i < 2, 6 - i, 3 - i)
        target = at(x, jnp.where(i < 2, z - 1 - i, z + 4 - i))
        return remote(away.at[t], inb.at[t, slot], f_ss.at[t], in_rs.at[t, slot], target)

    def pass_right(t, k):
        return remote(inb.at[t, k - 1], inb.at[t, k], in_ss.at[t, k - 1, 0], in_rs.at[t, k], right)

    def pass_left(t, k):
        return remote(inb.at[t, 7 - k], inb.at[t, 6 - k], in_ss.at[t, 7 - k, 1], in_rs.at[t, 6 - k], left)

    def arrival(t, slot):
        return remote(inb.at[t, slot], inb.at[t, slot], in_ss.at[t, slot, 0], in_rs.at[t, slot], right)

    def has_l(k):
        return (k >= 1) & (k <= i + 2)

    def has_r(k):
        return (k >= 1) & (k <= 5 - i)

    def z_start(t):
        for d in (1, 3, 2):
            x_arrival(t, d).wait_recv()

        @pl.loop(0, chunks)
        def _(c):
            inb[t, OWN, :, cols(c)] = nn(q[h], xr[t, :, cols(c)]).astype(bf16)
            away[t, :, cols(c)] = nn(q[1 - h], xr[t, :, cols(c)]).astype(bf16)

        @pl.when(i < 3)
        def _():
            own_right(t).start()

        @pl.when(i > 0)
        def _():
            own_left(t).start()

        own_away(t).start()

    def z_step(t, k):
        @pl.when(has_l(k))
        def _():
            arrival(t, k - 1).wait_recv()

            @pl.when(i < 3)
            def _():
                pass_right(t, k).start()

        @pl.when(has_r(k))
        def _():
            arrival(t, 7 - k).wait_recv()

            @pl.when(i > 0)
            def _():
                pass_left(t, k).start()

    def expert_forward(slot):
        gate = nn(inb[0, slot], wg[...])
        up = nn(inb[0, slot], wu[...])
        hidden = (gate * jax.nn.sigmoid(gate) * up).astype(bf16)

        @pl.loop(0, chunks)
        def _(c):
            part[0, slot, :, cols(c)] = nn(hidden, wd[:, cols(c)]).astype(bf16)

    def expert_backward(slot):
        gate = nn(inb[1, slot], wg[...])
        up = nn(inb[1, slot], wu[...])
        d_hidden = nt(inb[2, slot], wd[...])
        s = jax.nn.sigmoid(gate)
        d_gate = (d_hidden * up * s * (1.0 + gate * (1.0 - s))).astype(bf16)
        d_up = (d_hidden * gate * s).astype(bf16)

        @pl.loop(0, chunks)
        def _(c):
            part[1, slot, :, cols(c)] = (nt(d_gate, wg[cols(c), :]) + nt(d_up, wu[cols(c), :])).astype(bf16)

    def work(expert, k):
        @pl.loop(0, 2)
        def _(side):
            good = jnp.where(side == 0, has_l(k).astype(jnp.int32), ((k >= 0) & (k <= 5 - i)).astype(jnp.int32))

            @pl.when(good == 1)
            def _():
                expert(jnp.where(side == 0, k - 1, 7 - k))

    def back_left(o, k):
        slot = jnp.where(i == 0, AWAY, jnp.where(k >= 2, k - 2, FROM_RIGHT))
        return remote(
            part.at[o, k - 1], back.at[o, slot], o_ss.at[o, k - 1], o_rs.at[o, slot],
            at(x, jnp.where(i == 0, z - k, z - 1)),
        )

    def back_right(o, k):
        slot = jnp.where(i == 3, AWAY, jnp.where(k >= 2, 8 - k, FROM_LEFT))
        return remote(
            part.at[o, 7 - k], back.at[o, slot], o_ss.at[o, 7 - k], o_rs.at[o, slot],
            at(x, jnp.where(i == 3, z + k, z + 1)),
        )

    def returned(o, slot):
        return remote(back.at[o, slot], back.at[o, slot], o_ss.at[o, 0], o_rs.at[o, slot], right)

    def add_in(o, slot, src):
        returned(o, src).wait_recv()

        @pl.loop(0, chunks)
        def _(c):
            part[o, slot, :, cols(c)] = (
                part[o, slot, :, cols(c)].astype(f32) + back[o, src, :, cols(c)].astype(f32)
            ).astype(bf16)

    def back_step(o, n):
        kl = n - LAG * (3 - i)

        @pl.when(has_l(kl))
        def _():
            @pl.when(i < 3)
            def _():
                add_in(o, kl - 1, kl - 1)

            back_left(o, kl).start()

        kr = n - LAG * i

        @pl.when(has_r(kr))
        def _():
            @pl.when(i > 0)
            def _():
                add_in(o, 7 - kr, 7 - kr)

            back_right(o, kr).start()

    def y_copy(o, d):
        return remote(ys.at[o, d - 1], yr.at[o, rows48(x), :], y_ss.at[o, d - 1], y_rs.at[o, d - 1], at(x + d, z))

    def y_arrival(o, d):
        return remote(
            ys.at[o, d - 1], yr.at[o, rows48((x + NX - d) % NX), :], y_ss.at[o, d - 1], y_rs.at[o, d - 1], at(x + d, z)
        )

    def y_send(o):
        @pl.when(i > 0)
        def _():
            add_in(o, OWN, FROM_LEFT)

        @pl.when(i < 3)
        def _():
            add_in(o, OWN, FROM_RIGHT)

        returned(o, AWAY).wait_recv()
        for d in (2, 1, 3, 0):
            xd = (x + d) % NX

            @pl.loop(0, chunks)
            def _(c, d=d, xd=xd):
                picked = (
                    nn(qt[h, rows48(xd), :], part[o, OWN, :, cols(c)])
                    + nn(qt[1 - h, rows48(xd), :], back[o, AWAY, :, cols(c)])
                ).astype(bf16)
                if d == 0:
                    yr[o, rows48(x), cols(c)] = picked
                else:
                    ys[o, d - 1, :, cols(c)] = picked

            if d:
                y_copy(o, d).start()

    def pp_copy(o):
        if o == 0:
            return remote(sec.at[0], out_f, pp_ss.at[0], pp_rs.at[0], pp_up)
        return remote(sec.at[1], out_b, pp_ss.at[1], pp_rs.at[1], pp_down)

    def finish(o, pt_ref):
        for d in (1, 3, 2):
            y_arrival(o, d).wait_recv()

        @pl.loop(0, chunks)
        def _(c):
            expert_out = nn(pt_ref[...], yr[o, :, cols(c)]).astype(bf16).astype(f32)
            if o == 0:
                sec[o, :, cols(c)] = (tok[0, :, cols(c)].astype(f32) + fw[...] * expert_out).astype(bf16)
            else:
                sec[o, :, cols(c)] = (tok[3, :, cols(c)].astype(f32) + expert_out).astype(bf16)

        pp_copy(o).start()

    loads[0].wait()
    x_send(0, pf)
    loads[1].wait()
    x_send(1, pb)
    loads[2].wait()
    x_send(2, pb)
    z_start(0)
    for j in range(3, 7):
        loads[j].wait()

    last = B_AT + 5 + 3 * LAG

    @pl.loop(0, last + 1)
    def _(n):
        kb = n - B_AT

        @pl.when((n >= 1) & (n <= 5))
        def _():
            z_step(0, n)

        @pl.when(n == B_PREP)
        def _():
            z_start(1)
            z_start(2)

        @pl.when((kb >= 1) & (kb <= 5))
        def _():
            z_step(1, kb)
            z_step(2, kb)

        @pl.when(n <= 5)
        def _():
            work(expert_forward, n)

        @pl.when((kb >= 0) & (kb <= 5))
        def _():
            work(expert_backward, kb)

        back_step(0, n)
        back_step(1, kb)

        @pl.when(n == F_DONE)
        def _():
            y_send(0)

    finish(0, pft)
    y_send(1)
    finish(1, pbt)

    for t in range(3):
        for d in (1, 2, 3):
            x_copy(t, d).wait_send()
        own_away(t).wait_send()

        @pl.when(i < 3)
        def _(t=t):
            own_right(t).wait_send()

        @pl.when(i > 0)
        def _(t=t):
            own_left(t).wait_send()

    @pl.loop(1, 6)
    def _(k):
        for t in range(3):
            @pl.when(has_l(k) & (i < 3))
            def _(t=t):
                pass_right(t, k).wait_send()

            @pl.when(has_r(k) & (i > 0))
            def _(t=t):
                pass_left(t, k).wait_send()

        for o in range(2):
            @pl.when(has_l(k))
            def _(o=o):
                back_left(o, k).wait_send()

            @pl.when(has_r(k))
            def _(o=o):
                back_right(o, k).wait_send()

    for o in range(2):
        for d in (1, 2, 3):
            y_copy(o, d).wait_send()
        pp_copy(o).wait_send()
        pp_copy(o).wait_recv()


def slots(chosen, experts):
    count = chosen.shape[0]
    onehot = (chosen[:, None] == jnp.arange(experts, dtype=jnp.int32)[None, :]).astype(bf16)
    earlier = (jnp.arange(count)[:, None] > jnp.arange(count)[None, :]).astype(bf16)
    before = jnp.dot(earlier, onehot, preferred_element_type=f32)
    rank = jnp.sum(before * onehot.astype(f32), axis=1).astype(jnp.int32)
    place = (chosen // 2) * MSG + (chosen % 2) * CAP + rank
    spots = jnp.arange(NX * MSG, dtype=jnp.int32)
    spread = (spots[:, None] == place[None, :]).astype(bf16)
    gather = (place[:, None] == spots[None, :]).astype(bf16)
    return onehot, spread, gather


def routing_weight(tokens, router, onehot):
    logits = jnp.dot(tokens.astype(f32), router, precision=lax.Precision.HIGHEST)
    picked = jnp.sum(jnp.where(onehot > 0, logits, 0.0), axis=1)
    return route_scale * jax.nn.sigmoid(picked)


def per_device(fwd_in, fwd_ids, saved_in, bwd_ids, grad_in, router, w_gate, w_up, w_down):
    experts = router.shape[-1]
    tokens, width = fwd_in.shape[1:]
    units = w_down.shape[1]
    assert lax.axis_size("ep") == NX * NZ and experts == 2 * NX and tokens == 128
    fwd_hot, pf, pft = slots(fwd_ids[0, :, 0], experts)
    bwd_hot, pb, pbt = slots(bwd_ids[0, :, 0], experts)
    fwd_weight = routing_weight(fwd_in[0], router[0], fwd_hot)
    bwd_weight = routing_weight(saved_in[0], router[0], bwd_hot)
    weighted = (bwd_weight[:, None] * grad_in[0].astype(f32)).astype(bf16)
    block_row = jnp.arange(BLK)
    wide = jnp.arange(NX * MSG)
    source = (block_row // CAP) * MSG + block_row % CAP
    half = jnp.arange(2) * CAP
    q = (source[None, :, None] + half[:, None, None] == wide[None, None, :]).astype(bf16)
    qt = (source[None, None, :] + half[:, None, None] == wide[None, :, None]).astype(bf16)
    shape = jax.ShapeDtypeStruct((tokens, width), bf16)
    vmem = pl.BlockSpec(memory_space=pltpu.VMEM)
    hbm = pl.BlockSpec(memory_space=pl.ANY)
    dma = pltpu.SemaphoreType.DMA
    out_f, out_b = pl.pallas_call(
        kernel,
        out_shape=(shape, shape),
        in_specs=[vmem] * 7 + [hbm] * 7,
        out_specs=(hbm, hbm),
        scratch_shapes=[
            pltpu.VMEM((4, tokens, width), bf16),
            pltpu.VMEM((width, units), bf16),
            pltpu.VMEM((width, units), bf16),
            pltpu.VMEM((units, width), bf16),
            pltpu.VMEM((3, NX - 1, MSG, width), bf16),
            pltpu.VMEM((3, NX * MSG, width), bf16),
            pltpu.VMEM((3, 8, BLK, width), bf16),
            pltpu.VMEM((3, BLK, width), bf16),
            pltpu.VMEM((2, 8, BLK, width), bf16),
            pltpu.VMEM((2, 10, BLK, width), bf16),
            pltpu.VMEM((2, NX - 1, MSG, width), bf16),
            pltpu.VMEM((2, NX * MSG, width), bf16),
            pltpu.VMEM((2, tokens, width), bf16),
            dma((7,)),
            dma((3, NX - 1)),
            dma((3, NX - 1)),
            dma((3, 8, 2)),
            dma((3, 8)),
            dma((3,)),
            dma((2, 8)),
            dma((2, 10)),
            dma((2, NX - 1)),
            dma((2, NX - 1)),
            dma((2,)),
            dma((2,)),
        ],
        compiler_params=pltpu.CompilerParams(
            collective_id=0, has_side_effects=True, vmem_limit_bytes=67043328
        ),
        name="relay",
    )(
        pf, pb, pft, pbt, q, qt, fwd_weight[:, None],
        fwd_in[0], saved_in[0], weighted, grad_in[0], w_gate[0], w_up[0], w_down[0],
    )
    return out_f[None], out_b[None]


def solution(mesh):
    in_specs = (
        P("pp", "ep", None),
        P("pp", "ep", None),
        P("pp", "ep", None),
        P("pp", "ep", None),
        P("pp", "ep", None),
        P("pp", None, None),
        P("pp", None, "ep"),
        P("pp", None, "ep"),
        P("pp", "ep", None),
    )
    out_specs = (P("pp", "ep", None), P("pp", "ep", None))
    return jax.shard_map(
        per_device, mesh=mesh, in_specs=in_specs, out_specs=out_specs, check_vma=False
    )
```

```python
import functools

import jax
import jax.numpy as jnp
from jax import lax
from jax.experimental import pallas as pl
from jax.experimental.pallas import tpu as pltpu
from jax.sharding import PartitionSpec as P

route_scale = 2.5
MESH = pl.DeviceIdType.MESH
f32 = jnp.float32
bf16 = jnp.bfloat16

NX = 4
NZ = 8
SPAN = 4
CAP = 20
MSG = 48
BLK = NX * CAP
OWN = 7
FROM_LEFT, FROM_RIGHT, AWAY = 7, 8, 9
B_AT = 6
B_PREP = 3
LAG = 2
F_DONE = 12
COLS = 256
PARTS = 2


def nt(a, b):
    return lax.dot_general(a, b, (((1,), (1,)), ((), ())), preferred_element_type=f32)


def nn(a, b):
    return jnp.dot(a, b, preferred_element_type=f32)


def kernel(
    ids_f, ids_b, router, fwd, sav, grd, wg_h, wu_h, wd_h,
    out_f, out_b,
    pf, pb, pft, pbt, q, qt, fw,
    tok, wg, wu, wd, xs, xr, inb, away, part, back, ys, yr, sec,
    ld_sem, x_ss, x_rs, in_ss, in_rs, f_ss, o_ss, o_rs, y_ss, y_rs, pp_ss, pp_rs,
):
    width = tok.shape[2]
    chunks = width // COLS
    steps = chunks // PARTS
    span = width // PARTS
    both = range(PARTS)
    pp = lax.axis_index("pp")
    ep = lax.axis_index("ep")
    n_pp = lax.axis_size("pp")
    x = ep // NZ
    z = ep % NZ
    h = z // SPAN
    i = z % SPAN

    def at(xx, zz):
        return {"ep": (xx % NX) * NZ + (zz + NZ) % NZ}

    right = at(x, z + 1)
    left = at(x, z - 1)
    pp_up = {"pp": (pp + 1) % n_pp}
    pp_down = {"pp": (pp + n_pp - 1) % n_pp}

    loads = [
        pltpu.make_async_copy(src, dst, ld_sem.at[j])
        for j, (src, dst) in enumerate([
            (fwd, tok.at[0]), (sav, tok.at[1]), (grd, tok.at[3]),
            (wg_h, wg), (wu_h, wu), (wd_h, wd),
        ])
    ]
    for load in loads:
        load.start()

    barrier = pltpu.get_barrier_semaphore()
    friends = [at(x + 1, z), at(x + 2, z), at(x + 3, z), right, left, at(x, z + 2), at(x, z - 2), pp_up, pp_down]
    for friend in friends:
        pl.semaphore_signal(barrier, inc=1, device_id=friend, device_id_type=MESH)
    def remote(src, dst, ss, rs, dev):
        return pltpu.make_async_remote_copy(
            src_ref=src, dst_ref=dst, send_sem=ss, recv_sem=rs, device_id=dev, device_id_type=MESH
        )

    def cols(c):
        return pl.ds(pl.multiple_of(c * COLS, COLS), COLS)

    def cut(c):
        return pl.ds(c * span, span)

    def cut_cols(c, j):
        return pl.ds(pl.multiple_of(c * span + j * COLS, COLS), COLS)

    def rows48(k):
        return pl.ds(pl.multiple_of(k * MSG, 16), MSG)

    def iota(shape, axis):
        return lax.broadcasted_iota(jnp.int32, shape, axis).astype(f32)

    def ones(where):
        return jnp.where(where, 1.0, 0.0)

    def chosen(ids):
        count = ids.shape[1]
        same = iota((count, count), 0) == iota((count, count), 1)
        column = jnp.sum(jnp.where(same, ids[...].astype(f32), 0.0), axis=1, keepdims=True)
        return column == iota((count, 2 * NX), 1)

    def spots(ids, spread, gather):
        count = ids.shape[1]
        hot = ones(chosen(ids))
        earlier = ones(iota((count, count), 0) > iota((count, count), 1))
        before = nn(earlier.astype(bf16), hot.astype(bf16))
        expert = lax.broadcasted_iota(jnp.int32, (count, 2 * NX), 1)
        base = ((expert // 2) * MSG + (expert % 2) * CAP).astype(f32)
        place = jnp.sum(hot * (before + base), axis=1, keepdims=True)
        same = iota((count, count), 0) == iota((count, count), 1)
        place_row = jnp.sum(jnp.where(same, place, 0.0), axis=0, keepdims=True)
        gather[...] = ones(iota(gather.shape, 1) == place).astype(bf16)
        spread[...] = ones(iota(spread.shape, 0) == place_row).astype(bf16)

    def routing_weight(ids, t):
        count = ids.shape[1]
        logits = jnp.zeros((count, 2 * NX), f32)
        for c in range(width // 512):
            here = slice(c * 512, (c + 1) * 512)
            logits += lax.dot_general(
                tok[t, :, here].astype(f32), router[:, here], (((1,), (1,)), ((), ())),
                precision=lax.Precision.HIGHEST, preferred_element_type=f32,
            )
        logit = jnp.sum(jnp.where(chosen(ids), logits, 0.0), axis=1, keepdims=True)
        return route_scale * jax.nn.sigmoid(logit)

    def block_rows(shape, axis):
        row = iota(shape, axis)
        source = ones(row >= CAP) + ones(row >= 2 * CAP) + ones(row >= 3 * CAP)
        return row + (MSG - CAP) * source

    def block_picks():
        for half in range(2):
            shape = (BLK, NX * MSG)
            q[half] = ones(block_rows(shape, 0) + half * CAP == iota(shape, 1)).astype(bf16)
            shape = (NX * MSG, BLK)
            qt[half] = ones(block_rows(shape, 1) + half * CAP == iota(shape, 0)).astype(bf16)

    def x_copy(t, d, c):
        return remote(
            xs.at[t, d - 1, :, cut(c)], xr.at[t, rows48(x), cut(c)],
            x_ss.at[t, d - 1, c], x_rs.at[t, d - 1, c], at(x + d, z),
        )

    def x_arrival(t, d, c):
        return remote(
            xs.at[t, d - 1, :, cut(c)], xr.at[t, rows48((x + NX - d) % NX), cut(c)],
            x_ss.at[t, d - 1, c], x_rs.at[t, d - 1, c], at(x + d, z),
        )

    def x_send(t, p_ref):
        for c in both:
            for d in (2, 1, 3, 0):
                xd = (x + d) % NX

                @pl.loop(0, steps)
                def _(j, c=c, d=d, xd=xd):
                    picked = nn(p_ref[rows48(xd), :], tok[t, :, cut_cols(c, j)]).astype(bf16)
                    if d == 0:
                        xr[t, rows48(x), cut_cols(c, j)] = picked
                    else:
                        xs[t, d - 1, :, cut_cols(c, j)] = picked

                if d:
                    x_copy(t, d, c).start()

    def own_right(t, c):
        return remote(
            inb.at[t, OWN, :, cut(c)], inb.at[t, 0, :, cut(c)], in_ss.at[t, OWN, 0, c], in_rs.at[t, 0, c], right
        )

    def own_left(t, c):
        return remote(
            inb.at[t, OWN, :, cut(c)], inb.at[t, 6, :, cut(c)], in_ss.at[t, OWN, 1, c], in_rs.at[t, 6, c], left
        )

    def own_away(t, c):
        slot = jnp.where(i < 2, 6 - i, 3 - i)
        target = at(x, jnp.where(i < 2, z - 1 - i, z + 4 - i))
        return remote(away.at[t, :, cut(c)], inb.at[t, slot, :, cut(c)], f_ss.at[t, c], in_rs.at[t, slot, c], target)

    def pass_right(t, k, c):
        return remote(
            inb.at[t, k - 1, :, cut(c)], inb.at[t, k, :, cut(c)], in_ss.at[t, k - 1, 0, c], in_rs.at[t, k, c], right
        )

    def pass_left(t, k, c):
        return remote(
            inb.at[t, 7 - k, :, cut(c)], inb.at[t, 6 - k, :, cut(c)],
            in_ss.at[t, 7 - k, 1, c], in_rs.at[t, 6 - k, c], left,
        )

    def arrival(t, slot, c):
        here = inb.at[t, slot, :, cut(c)]
        return remote(here, here, in_ss.at[t, slot, 0, c], in_rs.at[t, slot, c], right)

    def has_l(k):
        return (k >= 1) & (k <= i + 2)

    def has_r(k):
        return (k >= 1) & (k <= 5 - i)

    def z_start(t):
        for c in both:
            for d in (1, 3, 2):
                x_arrival(t, d, c).wait_recv()

            @pl.loop(0, steps)
            def _(j, c=c):
                inb[t, OWN, :, cut_cols(c, j)] = nn(q[h], xr[t, :, cut_cols(c, j)]).astype(bf16)
                away[t, :, cut_cols(c, j)] = nn(q[1 - h], xr[t, :, cut_cols(c, j)]).astype(bf16)

            @pl.when(i < 3)
            def _(c=c):
                own_right(t, c).start()

            @pl.when(i > 0)
            def _(c=c):
                own_left(t, c).start()

            own_away(t, c).start()

    def z_step(t, k):
        for c in both:
            @pl.when(has_l(k))
            def _(c=c):
                arrival(t, k - 1, c).wait_recv()

                @pl.when(i < 3)
                def _():
                    pass_right(t, k, c).start()

            @pl.when(has_r(k))
            def _(c=c):
                arrival(t, 7 - k, c).wait_recv()

                @pl.when(i > 0)
                def _():
                    pass_left(t, k, c).start()

    def expert_forward(slot):
        gate = nn(inb[0, slot], wg[...])
        up = nn(inb[0, slot], wu[...])
        hidden = (gate * jax.nn.sigmoid(gate) * up).astype(bf16)

        @pl.loop(0, chunks)
        def _(c):
            part[0, slot, :, cols(c)] = nn(hidden, wd[:, cols(c)]).astype(bf16)

    def expert_backward(slot):
        gate = nn(inb[1, slot], wg[...])
        up = nn(inb[1, slot], wu[...])
        d_hidden = nt(inb[2, slot], wd[...])
        s = jax.nn.sigmoid(gate)
        d_gate = (d_hidden * up * s * (1.0 + gate * (1.0 - s))).astype(bf16)
        d_up = (d_hidden * gate * s).astype(bf16)

        @pl.loop(0, chunks)
        def _(c):
            part[1, slot, :, cols(c)] = (nt(d_gate, wg[cols(c), :]) + nt(d_up, wu[cols(c), :])).astype(bf16)

    def work(expert, k):
        @pl.loop(0, 2)
        def _(side):
            good = jnp.where(side == 0, has_l(k).astype(jnp.int32), ((k >= 0) & (k <= 5 - i)).astype(jnp.int32))

            @pl.when(good == 1)
            def _():
                expert(jnp.where(side == 0, k - 1, 7 - k))

    def back_left(o, k, c):
        slot = jnp.where(i == 0, AWAY, jnp.where(k >= 2, k - 2, FROM_RIGHT))
        return remote(
            part.at[o, k - 1, :, cut(c)], back.at[o, slot, :, cut(c)], o_ss.at[o, k - 1, c], o_rs.at[o, slot, c],
            at(x, jnp.where(i == 0, z - k, z - 1)),
        )

    def back_right(o, k, c):
        slot = jnp.where(i == 3, AWAY, jnp.where(k >= 2, 8 - k, FROM_LEFT))
        return remote(
            part.at[o, 7 - k, :, cut(c)], back.at[o, slot, :, cut(c)], o_ss.at[o, 7 - k, c], o_rs.at[o, slot, c],
            at(x, jnp.where(i == 3, z + k, z + 1)),
        )

    def returned(o, slot, c):
        here = back.at[o, slot, :, cut(c)]
        return remote(here, here, o_ss.at[o, 0, c], o_rs.at[o, slot, c], right)

    def add_in(o, slot, src, c):
        returned(o, src, c).wait_recv()

        @pl.loop(0, steps)
        def _(j):
            part[o, slot, :, cut_cols(c, j)] = (
                part[o, slot, :, cut_cols(c, j)].astype(f32) + back[o, src, :, cut_cols(c, j)].astype(f32)
            ).astype(bf16)

    def back_step(o, n):
        kl = n - LAG * (3 - i)
        kr = n - LAG * i
        for c in both:
            @pl.when(has_l(kl))
            def _(c=c):
                @pl.when(i < 3)
                def _():
                    add_in(o, kl - 1, kl - 1, c)

                back_left(o, kl, c).start()

            @pl.when(has_r(kr))
            def _(c=c):
                @pl.when(i > 0)
                def _():
                    add_in(o, 7 - kr, 7 - kr, c)

                back_right(o, kr, c).start()

    def y_copy(o, d, c):
        return remote(
            ys.at[o, d - 1, :, cut(c)], yr.at[o, rows48(x), cut(c)],
            y_ss.at[o, d - 1, c], y_rs.at[o, d - 1, c], at(x + d, z),
        )

    def y_arrival(o, d, c):
        return remote(
            ys.at[o, d - 1, :, cut(c)], yr.at[o, rows48((x + NX - d) % NX), cut(c)],
            y_ss.at[o, d - 1, c], y_rs.at[o, d - 1, c], at(x + d, z),
        )

    def y_send(o):
        for c in both:
            @pl.when(i > 0)
            def _(c=c):
                add_in(o, OWN, FROM_LEFT, c)

            @pl.when(i < 3)
            def _(c=c):
                add_in(o, OWN, FROM_RIGHT, c)

            returned(o, AWAY, c).wait_recv()
            for d in (2, 1, 3, 0):
                xd = (x + d) % NX

                @pl.loop(0, steps)
                def _(j, c=c, d=d, xd=xd):
                    picked = (
                        nn(qt[h, rows48(xd), :], part[o, OWN, :, cut_cols(c, j)])
                        + nn(qt[1 - h, rows48(xd), :], back[o, AWAY, :, cut_cols(c, j)])
                    ).astype(bf16)
                    if d == 0:
                        yr[o, rows48(x), cut_cols(c, j)] = picked
                    else:
                        ys[o, d - 1, :, cut_cols(c, j)] = picked

                if d:
                    y_copy(o, d, c).start()

    def pp_copy(o, c):
        if o == 0:
            return remote(sec.at[0, :, cut(c)], out_f.at[:, cut(c)], pp_ss.at[0, c], pp_rs.at[0, c], pp_up)
        return remote(sec.at[1, :, cut(c)], out_b.at[:, cut(c)], pp_ss.at[1, c], pp_rs.at[1, c], pp_down)

    def finish(o, pt_ref):
        for c in both:
            for d in (1, 3, 2):
                y_arrival(o, d, c).wait_recv()

            @pl.loop(0, steps)
            def _(j, c=c):
                here = cut_cols(c, j)
                expert_out = nn(pt_ref[...], yr[o, :, here]).astype(bf16).astype(f32)
                if o == 0:
                    sec[o, :, here] = (tok[0, :, here].astype(f32) + fw[...] * expert_out).astype(bf16)
                else:
                    sec[o, :, here] = (tok[3, :, here].astype(f32) + expert_out).astype(bf16)

            pp_copy(o, c).start()

    spots(ids_f, pf, pft)
    pl.semaphore_wait(barrier, len(friends))
    loads[0].wait()
    x_send(0, pf)
    spots(ids_b, pb, pbt)
    block_picks()
    loads[1].wait()
    x_send(1, pb)
    loads[2].wait()
    back_weight = routing_weight(ids_b, 1)
    for c in range(width // 512):
        here = slice(c * 512, (c + 1) * 512)
        tok[2, :, here] = (back_weight * tok[3, :, here].astype(f32)).astype(bf16)
    z_start(0)
    x_send(2, pb)
    fw[...] = routing_weight(ids_f, 0)
    for j in range(3, 6):
        loads[j].wait()

    last = B_AT + 5 + 3 * LAG

    @pl.loop(0, last + 1)
    def _(n):
        kb = n - B_AT

        @pl.when((n >= 1) & (n <= 5))
        def _():
            z_step(0, n)

        @pl.when(n == B_PREP)
        def _():
            z_start(1)
            z_start(2)

        @pl.when((kb >= 1) & (kb <= 5))
        def _():
            z_step(1, kb)
            z_step(2, kb)

        @pl.when(n <= 5)
        def _():
            work(expert_forward, n)

        @pl.when((kb >= 0) & (kb <= 5))
        def _():
            work(expert_backward, kb)

        back_step(0, n)
        back_step(1, kb)

        @pl.when(n == F_DONE)
        def _():
            y_send(0)

        @pl.when(n == F_DONE + 2)
        def _():
            finish(0, pft)

    y_send(1)
    finish(1, pbt)

    for c in both:
        for t in range(3):
            for d in (1, 2, 3):
                x_copy(t, d, c).wait_send()
            own_away(t, c).wait_send()

            @pl.when(i < 3)
            def _(t=t, c=c):
                own_right(t, c).wait_send()

            @pl.when(i > 0)
            def _(t=t, c=c):
                own_left(t, c).wait_send()

    @pl.loop(1, 6)
    def _(k):
        for c in both:
            for t in range(3):
                @pl.when(has_l(k) & (i < 3))
                def _(t=t, c=c):
                    pass_right(t, k, c).wait_send()

                @pl.when(has_r(k) & (i > 0))
                def _(t=t, c=c):
                    pass_left(t, k, c).wait_send()

            for o in range(2):
                @pl.when(has_l(k))
                def _(o=o, c=c):
                    back_left(o, k, c).wait_send()

                @pl.when(has_r(k))
                def _(o=o, c=c):
                    back_right(o, k, c).wait_send()

    for c in both:
        for o in range(2):
            for d in (1, 2, 3):
                y_copy(o, d, c).wait_send()
            pp_copy(o, c).wait_send()
            pp_copy(o, c).wait_recv()


def per_device(fwd_in, fwd_ids, saved_in, bwd_ids, grad_in, router, w_gate, w_up, w_down):
    experts = router.shape[-1]
    tokens, width = fwd_in.shape[1:]
    units = w_down.shape[1]
    assert lax.axis_size("ep") == NX * NZ and experts == 2 * NX and tokens == 128
    shape = jax.ShapeDtypeStruct((tokens, width), bf16)
    vmem = pl.BlockSpec(memory_space=pltpu.VMEM)
    hbm = pl.BlockSpec(memory_space=pl.ANY)
    dma = pltpu.SemaphoreType.DMA
    out_f, out_b = pl.pallas_call(
        kernel,
        out_shape=(shape, shape),
        in_specs=[vmem] * 3 + [hbm] * 6,
        out_specs=(hbm, hbm),
        scratch_shapes=[
            pltpu.VMEM((NX * MSG, tokens), bf16),
            pltpu.VMEM((NX * MSG, tokens), bf16),
            pltpu.VMEM((tokens, NX * MSG), bf16),
            pltpu.VMEM((tokens, NX * MSG), bf16),
            pltpu.VMEM((2, BLK, NX * MSG), bf16),
            pltpu.VMEM((2, NX * MSG, BLK), bf16),
            pltpu.VMEM((tokens, 1), f32),
            pltpu.VMEM((4, tokens, width), bf16),
            pltpu.VMEM((width, units), bf16),
            pltpu.VMEM((width, units), bf16),
            pltpu.VMEM((units, width), bf16),
            pltpu.VMEM((3, NX - 1, MSG, width), bf16),
            pltpu.VMEM((3, NX * MSG, width), bf16),
            pltpu.VMEM((3, 8, BLK, width), bf16),
            pltpu.VMEM((3, BLK, width), bf16),
            pltpu.VMEM((2, 8, BLK, width), bf16),
            pltpu.VMEM((2, 10, BLK, width), bf16),
            pltpu.VMEM((2, NX - 1, MSG, width), bf16),
            pltpu.VMEM((2, NX * MSG, width), bf16),
            pltpu.VMEM((2, tokens, width), bf16),
            dma((6,)),
            dma((3, NX - 1, PARTS)),
            dma((3, NX - 1, PARTS)),
            dma((3, 8, 2, PARTS)),
            dma((3, 8, PARTS)),
            dma((3, PARTS)),
            dma((2, 8, PARTS)),
            dma((2, 10, PARTS)),
            dma((2, NX - 1, PARTS)),
            dma((2, NX - 1, PARTS)),
            dma((2, PARTS)),
            dma((2, PARTS)),
        ],
        compiler_params=pltpu.CompilerParams(
            collective_id=0, has_side_effects=True, vmem_limit_bytes=67043328
        ),
        name="relay",
    )(
        fwd_ids[0].T, bwd_ids[0].T, jnp.swapaxes(router[0], 0, 1),
        fwd_in[0], saved_in[0], grad_in[0], w_gate[0], w_up[0], w_down[0],
    )
    return out_f[None], out_b[None]


def solution(mesh):
    in_specs = (
        P("pp", "ep", None),
        P("pp", "ep", None),
        P("pp", "ep", None),
        P("pp", "ep", None),
        P("pp", "ep", None),
        P("pp", None, None),
        P("pp", None, "ep"),
        P("pp", None, "ep"),
        P("pp", "ep", None),
    )
    out_specs = (P("pp", "ep", None), P("pp", "ep", None))
    return jax.shard_map(
        per_device, mesh=mesh, in_specs=in_specs, out_specs=out_specs, check_vma=False
    )
```

```python
import functools

import jax
import jax.numpy as jnp
from jax import lax
from jax.experimental import pallas as pl
from jax.experimental.pallas import tpu as pltpu
from jax.sharding import PartitionSpec as P

route_scale = 2.5
MESH = pl.DeviceIdType.MESH
f32 = jnp.float32
bf16 = jnp.bfloat16

NX = 4
NZ = 8
SPAN = 4
CAP = 20
MSG = 48
BLK = NX * CAP
OWN = 7
FROM_LEFT, FROM_RIGHT, AWAY = 7, 8, 9
B_AT = 6
B_PREP = 3
LAG = 2
F_DONE = 12
COLS = 896
PARTS = 4


def nt(a, b):
    return lax.dot_general(a, b, (((1,), (1,)), ((), ())), preferred_element_type=f32)


def nn(a, b):
    return jnp.dot(a, b, preferred_element_type=f32)


def kernel(
    ids_f, ids_b, router, fwd, sav, grd, wg_h, wu_h, wd_h,
    out_f, out_b,
    pf, pb, pft, pbt, q, qt, fw,
    tok, wg, wu, wd, xs, xr, inb, away, part, back, ys, yr, sec,
    ld_sem, x_ss, x_rs, in_ss, in_rs, f_ss, o_ss, o_rs, y_ss, y_rs, pp_ss, pp_rs,
):
    width = tok.shape[2]
    chunks = width // COLS
    steps = chunks // PARTS
    span = width // PARTS
    both = range(PARTS)
    pp = lax.axis_index("pp")
    ep = lax.axis_index("ep")
    n_pp = lax.axis_size("pp")
    x = ep // NZ
    z = ep % NZ
    h = z // SPAN
    i = z % SPAN

    def at(xx, zz):
        return {"ep": (xx % NX) * NZ + (zz + NZ) % NZ}

    right = at(x, z + 1)
    left = at(x, z - 1)
    pp_up = {"pp": (pp + 1) % n_pp}
    pp_down = {"pp": (pp + n_pp - 1) % n_pp}

    loads = [
        pltpu.make_async_copy(src, dst, ld_sem.at[j])
        for j, (src, dst) in enumerate([
            (fwd, tok.at[0]), (sav, tok.at[1]), (grd, tok.at[3]),
            (wg_h, wg), (wu_h, wu), (wd_h, wd),
        ])
    ]
    for load in loads:
        load.start()

    barrier = pltpu.get_barrier_semaphore()
    friends = [at(x + 1, z), at(x + 2, z), at(x + 3, z), right, left, at(x, z + 2), at(x, z - 2), pp_up, pp_down]
    for friend in friends:
        pl.semaphore_signal(barrier, inc=1, device_id=friend, device_id_type=MESH)
    def remote(src, dst, ss, rs, dev):
        return pltpu.make_async_remote_copy(
            src_ref=src, dst_ref=dst, send_sem=ss, recv_sem=rs, device_id=dev, device_id_type=MESH
        )

    def cols(c):
        return pl.ds(pl.multiple_of(c * COLS, COLS), COLS)

    def cut(c):
        return pl.ds(c * span, span)

    def cut_cols(c, j):
        return pl.ds(pl.multiple_of(c * span + j * COLS, COLS), COLS)

    def rows48(k):
        return pl.ds(pl.multiple_of(k * MSG, 16), MSG)

    def iota(shape, axis):
        return lax.broadcasted_iota(jnp.int32, shape, axis).astype(f32)

    def ones(where):
        return jnp.where(where, 1.0, 0.0)

    def chosen(ids):
        count = ids.shape[1]
        same = iota((count, count), 0) == iota((count, count), 1)
        column = jnp.sum(jnp.where(same, ids[...].astype(f32), 0.0), axis=1, keepdims=True)
        return column == iota((count, 2 * NX), 1)

    def spots(ids, spread, gather):
        count = ids.shape[1]
        hot = ones(chosen(ids))
        earlier = ones(iota((count, count), 0) > iota((count, count), 1))
        before = nn(earlier.astype(bf16), hot.astype(bf16))
        expert = lax.broadcasted_iota(jnp.int32, (count, 2 * NX), 1)
        base = ((expert // 2) * MSG + (expert % 2) * CAP).astype(f32)
        place = jnp.sum(hot * (before + base), axis=1, keepdims=True)
        same = iota((count, count), 0) == iota((count, count), 1)
        place_row = jnp.sum(jnp.where(same, place, 0.0), axis=0, keepdims=True)
        gather[...] = ones(iota(gather.shape, 1) == place).astype(bf16)
        spread[...] = ones(iota(spread.shape, 0) == place_row).astype(bf16)

    def routing_weight(ids, t):
        count = ids.shape[1]
        logits = jnp.zeros((count, 2 * NX), f32)
        for c in range(width // 512):
            here = slice(c * 512, (c + 1) * 512)
            logits += lax.dot_general(
                tok[t, :, here].astype(f32), router[:, here], (((1,), (1,)), ((), ())),
                precision=lax.Precision.HIGHEST, preferred_element_type=f32,
            )
        logit = jnp.sum(jnp.where(chosen(ids), logits, 0.0), axis=1, keepdims=True)
        return route_scale * jax.nn.sigmoid(logit)

    def block_rows(shape, axis):
        row = iota(shape, axis)
        source = ones(row >= CAP) + ones(row >= 2 * CAP) + ones(row >= 3 * CAP)
        return row + (MSG - CAP) * source

    def block_picks():
        for half in range(2):
            shape = (BLK, NX * MSG)
            q[half] = ones(block_rows(shape, 0) + half * CAP == iota(shape, 1)).astype(bf16)
            shape = (NX * MSG, BLK)
            qt[half] = ones(block_rows(shape, 1) + half * CAP == iota(shape, 0)).astype(bf16)

    def x_copy(t, d, c):
        return remote(
            xs.at[t, d - 1, :, cut(c)], xr.at[t, rows48(x), cut(c)],
            x_ss.at[t, d - 1, c], x_rs.at[t, d - 1, c], at(x + d, z),
        )

    def x_arrival(t, d, c):
        return remote(
            xs.at[t, d - 1, :, cut(c)], xr.at[t, rows48((x + NX - d) % NX), cut(c)],
            x_ss.at[t, d - 1, c], x_rs.at[t, d - 1, c], at(x + d, z),
        )

    def x_send(t, p_ref):
        for c in both:
            for d in (2, 1, 3, 0):
                xd = (x + d) % NX

                @pl.loop(0, steps)
                def _(j, c=c, d=d, xd=xd):
                    picked = nn(p_ref[rows48(xd), :], tok[t, :, cut_cols(c, j)]).astype(bf16)
                    if d == 0:
                        xr[t, rows48(x), cut_cols(c, j)] = picked
                    else:
                        xs[t, d - 1, :, cut_cols(c, j)] = picked

                if d:
                    x_copy(t, d, c).start()

    def own_right(t, c):
        return remote(
            inb.at[t, OWN, :, cut(c)], inb.at[t, 0, :, cut(c)], in_ss.at[t, OWN, 0, c], in_rs.at[t, 0, c], right
        )

    def own_left(t, c):
        return remote(
            inb.at[t, OWN, :, cut(c)], inb.at[t, 6, :, cut(c)], in_ss.at[t, OWN, 1, c], in_rs.at[t, 6, c], left
        )

    def own_away(t, c):
        slot = jnp.where(i < 2, 6 - i, 3 - i)
        target = at(x, jnp.where(i < 2, z - 1 - i, z + 4 - i))
        return remote(away.at[t, :, cut(c)], inb.at[t, slot, :, cut(c)], f_ss.at[t, c], in_rs.at[t, slot, c], target)

    def pass_right(t, k, c):
        return remote(
            inb.at[t, k - 1, :, cut(c)], inb.at[t, k, :, cut(c)], in_ss.at[t, k - 1, 0, c], in_rs.at[t, k, c], right
        )

    def pass_left(t, k, c):
        return remote(
            inb.at[t, 7 - k, :, cut(c)], inb.at[t, 6 - k, :, cut(c)],
            in_ss.at[t, 7 - k, 1, c], in_rs.at[t, 6 - k, c], left,
        )

    def arrival(t, slot, c):
        here = inb.at[t, slot, :, cut(c)]
        return remote(here, here, in_ss.at[t, slot, 0, c], in_rs.at[t, slot, c], right)

    def has_l(k):
        return (k >= 1) & (k <= i + 2)

    def has_r(k):
        return (k >= 1) & (k <= 5 - i)

    def z_start(t):
        for c in both:
            for d in (1, 3, 2):
                x_arrival(t, d, c).wait_recv()

            @pl.loop(0, steps)
            def _(j, c=c):
                inb[t, OWN, :, cut_cols(c, j)] = nn(q[h], xr[t, :, cut_cols(c, j)]).astype(bf16)
                away[t, :, cut_cols(c, j)] = nn(q[1 - h], xr[t, :, cut_cols(c, j)]).astype(bf16)

            @pl.when(i < 3)
            def _(c=c):
                own_right(t, c).start()

            @pl.when(i > 0)
            def _(c=c):
                own_left(t, c).start()

            own_away(t, c).start()

    def z_step(t, k):
        for c in both:
            @pl.when(has_l(k))
            def _(c=c):
                arrival(t, k - 1, c).wait_recv()

                @pl.when(i < 3)
                def _():
                    pass_right(t, k, c).start()

            @pl.when(has_r(k))
            def _(c=c):
                arrival(t, 7 - k, c).wait_recv()

                @pl.when(i > 0)
                def _():
                    pass_left(t, k, c).start()

    def expert_forward(slot):
        gate = nn(inb[0, slot], wg[...])
        up = nn(inb[0, slot], wu[...])
        hidden = (gate * jax.nn.sigmoid(gate) * up).astype(bf16)

        @pl.loop(0, chunks)
        def _(c):
            part[0, slot, :, cols(c)] = nn(hidden, wd[:, cols(c)]).astype(bf16)

    def expert_backward(slot):
        gate = nn(inb[1, slot], wg[...])
        up = nn(inb[1, slot], wu[...])
        d_hidden = nt(inb[2, slot], wd[...])
        s = jax.nn.sigmoid(gate)
        d_gate = (d_hidden * up * s * (1.0 + gate * (1.0 - s))).astype(bf16)
        d_up = (d_hidden * gate * s).astype(bf16)

        @pl.loop(0, chunks)
        def _(c):
            part[1, slot, :, cols(c)] = (nt(d_gate, wg[cols(c), :]) + nt(d_up, wu[cols(c), :])).astype(bf16)

    def work(expert, k):
        @pl.loop(0, 2)
        def _(side):
            good = jnp.where(side == 0, has_l(k).astype(jnp.int32), ((k >= 0) & (k <= 5 - i)).astype(jnp.int32))

            @pl.when(good == 1)
            def _():
                expert(jnp.where(side == 0, k - 1, 7 - k))

    def back_left(o, k, c):
        slot = jnp.where(i == 0, AWAY, jnp.where(k >= 2, k - 2, FROM_RIGHT))
        return remote(
            part.at[o, k - 1, :, cut(c)], back.at[o, slot, :, cut(c)], o_ss.at[o, k - 1, c], o_rs.at[o, slot, c],
            at(x, jnp.where(i == 0, z - k, z - 1)),
        )

    def back_right(o, k, c):
        slot = jnp.where(i == 3, AWAY, jnp.where(k >= 2, 8 - k, FROM_LEFT))
        return remote(
            part.at[o, 7 - k, :, cut(c)], back.at[o, slot, :, cut(c)], o_ss.at[o, 7 - k, c], o_rs.at[o, slot, c],
            at(x, jnp.where(i == 3, z + k, z + 1)),
        )

    def returned(o, slot, c):
        here = back.at[o, slot, :, cut(c)]
        return remote(here, here, o_ss.at[o, 0, c], o_rs.at[o, slot, c], right)

    def add_in(o, slot, src, c):
        returned(o, src, c).wait_recv()

        @pl.loop(0, steps)
        def _(j):
            part[o, slot, :, cut_cols(c, j)] = (
                part[o, slot, :, cut_cols(c, j)].astype(f32) + back[o, src, :, cut_cols(c, j)].astype(f32)
            ).astype(bf16)

    def back_step(o, n):
        kl = n - LAG * (3 - i)
        kr = n - LAG * i
        for c in both:
            @pl.when(has_l(kl))
            def _(c=c):
                @pl.when(i < 3)
                def _():
                    add_in(o, kl - 1, kl - 1, c)

                back_left(o, kl, c).start()

            @pl.when(has_r(kr))
            def _(c=c):
                @pl.when(i > 0)
                def _():
                    add_in(o, 7 - kr, 7 - kr, c)

                back_right(o, kr, c).start()

    def y_copy(o, d, c):
        return remote(
            ys.at[o, d - 1, :, cut(c)], yr.at[o, rows48(x), cut(c)],
            y_ss.at[o, d - 1, c], y_rs.at[o, d - 1, c], at(x + d, z),
        )

    def y_arrival(o, d, c):
        return remote(
            ys.at[o, d - 1, :, cut(c)], yr.at[o, rows48((x + NX - d) % NX), cut(c)],
            y_ss.at[o, d - 1, c], y_rs.at[o, d - 1, c], at(x + d, z),
        )

    def y_send(o):
        for c in both:
            @pl.when(i > 0)
            def _(c=c):
                add_in(o, OWN, FROM_LEFT, c)

            @pl.when(i < 3)
            def _(c=c):
                add_in(o, OWN, FROM_RIGHT, c)

            returned(o, AWAY, c).wait_recv()
            for d in (2, 1, 3, 0):
                xd = (x + d) % NX

                @pl.loop(0, steps)
                def _(j, c=c, d=d, xd=xd):
                    picked = (
                        nn(qt[h, rows48(xd), :], part[o, OWN, :, cut_cols(c, j)])
                        + nn(qt[1 - h, rows48(xd), :], back[o, AWAY, :, cut_cols(c, j)])
                    ).astype(bf16)
                    if d == 0:
                        yr[o, rows48(x), cut_cols(c, j)] = picked
                    else:
                        ys[o, d - 1, :, cut_cols(c, j)] = picked

                if d:
                    y_copy(o, d, c).start()

    def pp_copy(o, c):
        if o == 0:
            return remote(sec.at[0, :, cut(c)], out_f.at[:, cut(c)], pp_ss.at[0, c], pp_rs.at[0, c], pp_up)
        return remote(sec.at[1, :, cut(c)], out_b.at[:, cut(c)], pp_ss.at[1, c], pp_rs.at[1, c], pp_down)

    def finish(o, pt_ref):
        for c in both:
            for d in (1, 3, 2):
                y_arrival(o, d, c).wait_recv()

            @pl.loop(0, steps)
            def _(j, c=c):
                here = cut_cols(c, j)
                expert_out = nn(pt_ref[...], yr[o, :, here]).astype(bf16).astype(f32)
                if o == 0:
                    sec[o, :, here] = (tok[0, :, here].astype(f32) + fw[...] * expert_out).astype(bf16)
                else:
                    sec[o, :, here] = (tok[3, :, here].astype(f32) + expert_out).astype(bf16)

            pp_copy(o, c).start()

    spots(ids_f, pf, pft)
    pl.semaphore_wait(barrier, len(friends))
    loads[0].wait()
    x_send(0, pf)
    spots(ids_b, pb, pbt)
    block_picks()
    loads[1].wait()
    x_send(1, pb)
    loads[2].wait()
    back_weight = routing_weight(ids_b, 1)
    for c in range(width // 512):
        here = slice(c * 512, (c + 1) * 512)
        tok[2, :, here] = (back_weight * tok[3, :, here].astype(f32)).astype(bf16)
    z_start(0)
    x_send(2, pb)
    fw[...] = routing_weight(ids_f, 0)
    for j in range(3, 6):
        loads[j].wait()

    last = B_AT + 5 + 3 * LAG

    @pl.loop(0, last + 1)
    def _(n):
        kb = n - B_AT

        @pl.when((n >= 1) & (n <= 5))
        def _():
            z_step(0, n)

        @pl.when(n == B_PREP)
        def _():
            z_start(1)
            z_start(2)

        @pl.when((kb >= 1) & (kb <= 5))
        def _():
            z_step(1, kb)
            z_step(2, kb)

        @pl.when(n <= 5)
        def _():
            work(expert_forward, n)

        @pl.when((kb >= 0) & (kb <= 5))
        def _():
            work(expert_backward, kb)

        back_step(0, n)
        back_step(1, kb)

        @pl.when(n == F_DONE)
        def _():
            y_send(0)

        @pl.when(n == F_DONE + 2)
        def _():
            finish(0, pft)

    y_send(1)
    finish(1, pbt)

    for c in both:
        for t in range(3):
            for d in (1, 2, 3):
                x_copy(t, d, c).wait_send()
            own_away(t, c).wait_send()

            @pl.when(i < 3)
            def _(t=t, c=c):
                own_right(t, c).wait_send()

            @pl.when(i > 0)
            def _(t=t, c=c):
                own_left(t, c).wait_send()

    @pl.loop(1, 6)
    def _(k):
        for c in both:
            for t in range(3):
                @pl.when(has_l(k) & (i < 3))
                def _(t=t, c=c):
                    pass_right(t, k, c).wait_send()

                @pl.when(has_r(k) & (i > 0))
                def _(t=t, c=c):
                    pass_left(t, k, c).wait_send()

            for o in range(2):
                @pl.when(has_l(k))
                def _(o=o, c=c):
                    back_left(o, k, c).wait_send()

                @pl.when(has_r(k))
                def _(o=o, c=c):
                    back_right(o, k, c).wait_send()

    for c in both:
        for o in range(2):
            for d in (1, 2, 3):
                y_copy(o, d, c).wait_send()
            pp_copy(o, c).wait_send()
            pp_copy(o, c).wait_recv()


def per_device(fwd_in, fwd_ids, saved_in, bwd_ids, grad_in, router, w_gate, w_up, w_down):
    experts = router.shape[-1]
    tokens, width = fwd_in.shape[1:]
    units = w_down.shape[1]
    assert lax.axis_size("ep") == NX * NZ and experts == 2 * NX and tokens == 128
    shape = jax.ShapeDtypeStruct((tokens, width), bf16)
    vmem = pl.BlockSpec(memory_space=pltpu.VMEM)
    hbm = pl.BlockSpec(memory_space=pl.ANY)
    dma = pltpu.SemaphoreType.DMA
    out_f, out_b = pl.pallas_call(
        kernel,
        out_shape=(shape, shape),
        in_specs=[vmem] * 3 + [hbm] * 6,
        out_specs=(hbm, hbm),
        scratch_shapes=[
            pltpu.VMEM((NX * MSG, tokens), bf16),
            pltpu.VMEM((NX * MSG, tokens), bf16),
            pltpu.VMEM((tokens, NX * MSG), bf16),
            pltpu.VMEM((tokens, NX * MSG), bf16),
            pltpu.VMEM((2, BLK, NX * MSG), bf16),
            pltpu.VMEM((2, NX * MSG, BLK), bf16),
            pltpu.VMEM((tokens, 1), f32),
            pltpu.VMEM((4, tokens, width), bf16),
            pltpu.VMEM((width, units), bf16),
            pltpu.VMEM((width, units), bf16),
            pltpu.VMEM((units, width), bf16),
            pltpu.VMEM((3, NX - 1, MSG, width), bf16),
            pltpu.VMEM((3, NX * MSG, width), bf16),
            pltpu.VMEM((3, 8, BLK, width), bf16),
            pltpu.VMEM((3, BLK, width), bf16),
            pltpu.VMEM((2, 8, BLK, width), bf16),
            pltpu.VMEM((2, 10, BLK, width), bf16),
            pltpu.VMEM((2, NX - 1, MSG, width), bf16),
            pltpu.VMEM((2, NX * MSG, width), bf16),
            pltpu.VMEM((2, tokens, width), bf16),
            dma((6,)),
            dma((3, NX - 1, PARTS)),
            dma((3, NX - 1, PARTS)),
            dma((3, 8, 2, PARTS)),
            dma((3, 8, PARTS)),
            dma((3, PARTS)),
            dma((2, 8, PARTS)),
            dma((2, 10, PARTS)),
            dma((2, NX - 1, PARTS)),
            dma((2, NX - 1, PARTS)),
            dma((2, PARTS)),
            dma((2, PARTS)),
        ],
        compiler_params=pltpu.CompilerParams(
            collective_id=0, has_side_effects=True, vmem_limit_bytes=67043328
        ),
        name="relay",
    )(
        fwd_ids[0].T, bwd_ids[0].T, jnp.swapaxes(router[0], 0, 1),
        fwd_in[0], saved_in[0], grad_in[0], w_gate[0], w_up[0], w_down[0],
    )
    return out_f[None], out_b[None]


def solution(mesh):
    in_specs = (
        P("pp", "ep", None),
        P("pp", "ep", None),
        P("pp", "ep", None),
        P("pp", "ep", None),
        P("pp", "ep", None),
        P("pp", None, None),
        P("pp", None, "ep"),
        P("pp", None, "ep"),
        P("pp", "ep", None),
    )
    out_specs = (P("pp", "ep", None), P("pp", "ep", None))
    return jax.shard_map(
        per_device, mesh=mesh, in_specs=in_specs, out_specs=out_specs, check_vma=False
    )
```
